256 devices in a mesh: seq: 32 (over y, z), head: 4 (over x), dp: 2 (over core).
Axes of the slice: x: 4, y: 4, z: 8, core: 2. Of those that a mesh axis runs over, the one named last changes fastest.
Arguments:
- inputs: bfloat16 [2, 16384, 3584], P('dp', 'seq', 'head'), may hold values from -6 to 6
- value_weight: bfloat16 [3584, 3584], P(None, 'head'), may hold values from -0.09375 to 0.09375
- cotangent: bfloat16 [2, 16384, 3584], P('dp', 'seq', 'head'), may hold values from -6 to 6
- spikes_q: int32 [2, 16384, 3584], P('dp', 'seq', 'head'), may hold values from 0 to 3
- spikes_k: int32 [2, 16384, 3584], P('dp', 'seq', 'head'), may hold values from 0 to 3
- log_decay: float32 [2, 28, 16384], P('dp', 'head', 'seq'), may hold values from -1.0976562 to 0, as said below
Outputs:
- grad_input: bfloat16 [2, 16384, 3584], P('dp', 'seq', 'head')
- grad_weight: float32 [3584, 3584], P(('seq', 'dp'), 'head')
The draws below stay inside these ranges and needn't reach their ends.
Inputs may be any that keep to these rules, and one draw needn't show every extreme that they name: `spikes_q`: spike count of a token in a channel. `spikes_k`: spike count of a token in a channel. `log_decay`: negative.
All inputs are finite; a program needn't handle non-finite values.
Results may differ from the reference program's by a relative error of at most 0.0051.
Values may be sent and summed in bfloat16 or wider, within the bound.
A program may use at most 128 MiB of HBM per device.

```python
import math
import jax
import jax.numpy as jnp
from jax import lax

D = 3584
ATTENTION_COUNT = 28
HEAD_DIM = 128
TOK_DEV = 512
FEAT = 3584
BLOCK = 512
STRING_LENGTH = 16384
STRING_COUNT = 2


def draw_log_decay(key, part):
    string_currents = jax.random.split(key, 7)
    fast_share = 0.45
    fast_heads = jax.random.uniform(string_currents[0], (STRING_COUNT, ATTENTION_COUNT, 1), jnp.float32) < fast_share
    slow_rate = math.log(2.0) / STRING_LENGTH * jnp.exp(jax.random.uniform(string_currents[1], (STRING_COUNT, ATTENTION_COUNT, 1), jnp.float32, math.log(0.3), 0.0))
    fast_rate = 1.0 / (TOK_DEV * jax.random.uniform(string_currents[2], (STRING_COUNT, ATTENTION_COUNT, 1), jnp.float32, 0.06, 0.1))
    resting_frequency = jnp.where(fast_heads, fast_rate, slow_rate)
    position = jnp.arange(STRING_LENGTH).astype(jnp.float32)
    slope_scaling_factor = 0.5 + position / STRING_LENGTH
    roughness_measure = jnp.exp(jax.random.uniform(string_currents[3], (STRING_COUNT, ATTENTION_COUNT, STRING_LENGTH), jnp.float32, math.log(0.5), math.log(2.0)))
    leading_index = jax.random.randint(string_currents[4], (STRING_COUNT, 1, 1), 0, STRING_LENGTH)
    place_offset = jax.random.randint(string_currents[6], (STRING_COUNT, 1, 1), 1, STRING_LENGTH)
    trailing_index = (leading_index + place_offset) % STRING_LENGTH
    cluster_indices = jnp.concatenate([leading_index, trailing_index], axis=-1)
    spike_cluster_list = jnp.sum((jnp.arange(STRING_LENGTH)[None, None, :, None] == cluster_indices[:, :, None, :]).astype(jnp.float32), axis=-1)
    cluster_cost_factor = jax.random.uniform(string_currents[5], (STRING_COUNT, ATTENTION_COUNT, 1), jnp.float32, 0.2, 0.5)
    return -(resting_frequency * slope_scaling_factor[None, None, :] * roughness_measure) + spike_cluster_list * jnp.log(1.0 - cluster_cost_factor)


def set_ends(result, own_key, low, high):
    longest = result.shape.index(max(result.shape))
    spots = []
    for shift in (0, 1):
        where = [jax.random.randint(jax.random.fold_in(own_key, axis), (), 0, length) for axis, length in enumerate(result.shape)]
        where[longest] = (where[longest] + shift) % result.shape[longest]
        spots.append(tuple(where))
    return result.at[spots[0]].set(low).at[spots[1]].set(high)


def raised(values, key, source, target, shards_of, factor):
    def block_of(axis_at):
        return (jnp.arange(values.shape[axis_at]) // (values.shape[axis_at] // shards_of)).reshape((-1,) + (1,) * (values.ndim - 1 - axis_at))

    first = jax.random.permutation(key, shards_of)[block_of(target)]
    second = (block_of(target) + shards_of // 2) % shards_of
    return jnp.where((block_of(source) == first) | (block_of(source) == second), factor * values, values)


def block_scale(rng, shape, pieces, low, high):
    level, own = 1.0, jax.random.fold_in(rng, 6)
    for dim, blocks in pieces:
        draws = jnp.exp(jax.random.uniform(jax.random.fold_in(own, dim), (blocks,), jnp.float32, low / len(pieces), high / len(pieces)))
        level = level * jnp.repeat(draws, shape[dim] // blocks).reshape([-1 if axis == dim else 1 for axis in range(len(shape))])
    return level


def gaussian(key, extent, width, reach, cuts=(), dtype=jnp.bfloat16):
    drawn = width * jax.random.normal(key, extent, jnp.float32)
    if cuts:
        drawn = drawn * block_scale(key, extent, cuts, -0.22, 0.18)
    return jnp.clip(drawn, -reach, reach).astype(dtype)


def heavy_noise(rng, extent, scale, most, cuts, heavy, kind=jnp.bfloat16):
    drawn = scale * jax.random.normal(rng, extent, jnp.float32)
    if cuts:
        drawn = drawn * block_scale(rng, extent, cuts, -0.22, 0.18)
    return jnp.clip(raised(drawn, jax.random.fold_in(rng, 3), *heavy), -most, most).astype(kind)


def setup_inputs(seed: int = 0) -> dict:
    key_list = jax.random.split(jax.random.key(seed), 7)
    inputs = heavy_noise(key_list[0], (STRING_COUNT, STRING_LENGTH, D), 1.0, 6.0, ((0, 2), (1, 32), (2, 4)), (1, 2, 32, 2.75))
    value_weight = gaussian(key_list[1], (D, FEAT), D ** -0.5, 0.09375, ((1, 4),))
    cotangent = gaussian(key_list[2], (STRING_COUNT, STRING_LENGTH, FEAT), 1.0, 6.0, ((0, 2), (1, 32), (2, 4)))
    spikes_q = set_ends(jax.random.randint(key_list[3], (STRING_COUNT, STRING_LENGTH, FEAT), 0, 4), jax.random.fold_in(key_list[3], 1), 0, 3).astype(jnp.int32)
    spikes_k = set_ends(jax.random.randint(key_list[4], (STRING_COUNT, STRING_LENGTH, FEAT), 0, 4), jax.random.fold_in(key_list[4], 1), 0, 3).astype(jnp.int32)
    log_decay = draw_log_decay(jax.random.fold_in(key_list[6], 71), 0)
    return {"inputs": inputs, "value_weight": value_weight, "cotangent": cotangent, "spikes_q": spikes_q, "spikes_k": spikes_k, "log_decay": log_decay}


def head_grads(query_spikes, key_spikes, out_grads, log_rates):
    queries = query_spikes.astype(jnp.float32)
    keys_f = key_spikes.astype(jnp.float32)
    grads_f = out_grads.astype(jnp.float32)
    cumulative = jnp.cumsum(log_rates, axis=1)
    scores = jnp.einsum('ntd,nsd->nts', queries, keys_f, precision=lax.Precision.HIGHEST)
    causal = jnp.arange(BLOCK)[:, None] >= jnp.arange(BLOCK)[None, :]
    log_gaps = jnp.where(causal[None], cumulative[:, :, None] - cumulative[:, None, :], -jnp.inf)
    weighted = (scores * jnp.exp(log_gaps)).astype(jnp.bfloat16)
    local_part = jnp.einsum('nts,nte->nse', weighted.astype(jnp.float32), grads_f, precision=lax.Precision.HIGHEST)
    state_terms = jnp.einsum('ntd,nte->nde', queries * jnp.exp(cumulative)[:, :, None], grads_f, precision=lax.Precision.HIGHEST)
    block_decay = jnp.exp(cumulative[:, -1])

    def backward_step(carry_state, item):
        decay_now, term_now = item
        return (term_now + decay_now * carry_state, carry_state)
    _, carry_in = lax.scan(backward_step, jnp.zeros((HEAD_DIM, HEAD_DIM), jnp.float32), (block_decay, state_terms), reverse=True)
    carried = jnp.exp(cumulative[:, -1:] - cumulative)[:, :, None] * jnp.einsum('nsd,nde->nse', keys_f, carry_in, precision=lax.Precision.HIGHEST)
    return local_part + carried

def reference(inputs, value_weight, cotangent, spikes_q, spikes_k, log_decay):
    block_count = STRING_LENGTH // BLOCK
    grad_scale = 1.0 / (2.25 * HEAD_DIM * math.sqrt(STRING_LENGTH))
    weight_total = jnp.zeros((D, FEAT), jnp.float32)
    input_rows = []
    for sequence in range(STRING_COUNT):
        query_all = spikes_q[sequence].reshape(block_count, BLOCK, ATTENTION_COUNT, HEAD_DIM)
        key_all = spikes_k[sequence].reshape(block_count, BLOCK, ATTENTION_COUNT, HEAD_DIM)
        grad_all = cotangent[sequence].reshape(block_count, BLOCK, ATTENTION_COUNT, HEAD_DIM)
        rates_all = log_decay[sequence].reshape(ATTENTION_COUNT, block_count, BLOCK)

        def one_head(head_index):
            return head_grads(lax.dynamic_index_in_dim(query_all, head_index, 2, False), lax.dynamic_index_in_dim(key_all, head_index, 2, False), lax.dynamic_index_in_dim(grad_all, head_index, 2, False), lax.dynamic_index_in_dim(rates_all, head_index, 0, False))
        per_head = lax.map(one_head, jnp.arange(ATTENTION_COUNT).astype(jnp.int32))
        value_grad = (grad_scale * per_head).astype(jnp.bfloat16)
        value_grad = value_grad.transpose(1, 2, 0, 3).reshape(STRING_LENGTH, FEAT)
        input_rows.append(jnp.dot(value_grad, value_weight.T, preferred_element_type=jnp.float32).astype(jnp.bfloat16))
        weight_total = weight_total + jnp.dot(inputs[sequence].T, value_grad, preferred_element_type=jnp.float32)
    grad_input = jnp.stack(input_rows, axis=0)
    grad_weight = weight_total * (1.0 / math.sqrt(STRING_COUNT * STRING_LENGTH))
    return (grad_input, grad_weight)
```

```python
import math

import jax
import jax.numpy as jnp
from jax import lax
from jax.experimental import pallas as pl
from jax.experimental.pallas import tpu as pltpu
from jax.sharding import PartitionSpec as P

NX, NY, NZ = 4, 4, 8
T, F, H, E = 512, 896, 7, 128
HT = T // 2
HF = F // 2
ZR = F // NZ
OUT = ZR // 2
SL = E // NZ
YROWS = H * SL + 8
CUTS = ((0, 512), (512, 384))
BF, F32 = jnp.bfloat16, jnp.float32
MESH = pl.DeviceIdType.MESH

_names = {}
_count = 0
for _name, _n in (
    ("dz", 8), ("a1", 8), ("a2", 8), ("yx", 4), ("xd", 2), ("xp", 1), ("xf", 2), ("vg", 1),
    ("xh", 2), ("xs", 4), ("yh", 2), ("ys", 4), ("zp", 8), ("zm", 6), ("fp", 1),
):
    _names[_name] = _count
    _count += _n
NSEM = _count


def dot(a, b, ca, cb):
    return lax.dot_general(a, b, (((ca,), (cb,)), ((), ())), preferred_element_type=F32)


def kernel(
    grad_scale, weight_scale,
    x_hbm, w_hbm, g_hbm, q_hbm, k_hbm, ld_ref,
    gi_hbm, gw_hbm,
    wv, gv, qv, kv, xg, cumr, cumc, dzs, dzr, tsend, trecv, lbuf, ysend, yrecv, csend, crecv,
    loc, vgs, p2s, pss, pf, xh, xf, gio, dwf, dsend, yh, yf, zps, zpr, zms, zmr, fin, gwv,
    ss, rs, ls,
):
    s = lax.axis_index("seq")
    x = lax.axis_index("head")
    c = lax.axis_index("dp")
    y, z = lax.div(s, NZ), lax.rem(s, NZ)
    half_x, par_x = lax.div(x, 2), lax.rem(x, 2)
    half_y, par_y = lax.div(y, 2), lax.rem(y, 2)
    other = 1 - c
    xp, xm = lax.rem(x + 1, NX), lax.rem(x + NX - 1, NX)
    yp, ym = lax.rem(y + 1, NY), lax.rem(y + NY - 1, NY)
    zp, zm = lax.rem(z + 1, NZ), lax.rem(z + NZ - 1, NZ)

    def dev(yy=None, zz=None, xx=None, cc=None):
        yy = y if yy is None else yy
        zz = z if zz is None else zz
        return (yy * NZ + zz, x if xx is None else xx, c if cc is None else cc)

    def rcopy(src, dst, name, send, recv, to):
        base = _names[name]
        return pltpu.make_async_remote_copy(
            src_ref=src, dst_ref=dst, send_sem=ss.at[base + send], recv_sem=rs.at[base + recv],
            device_id=to, device_id_type=MESH,
        )

    loads = [
        pltpu.make_async_copy(q_hbm.at[0], qv, ls.at[0]),
        pltpu.make_async_copy(g_hbm.at[0], gv, ls.at[1]),
        pltpu.make_async_copy(k_hbm.at[0], kv, ls.at[2]),
        pltpu.make_async_copy(w_hbm, wv, ls.at[3]),
    ]
    for load in loads:
        load.start()

    barrier = pltpu.get_barrier_semaphore()
    greet = [dev(xx=xp, cc=c), dev(xx=xp, cc=other), dev(xx=xm, cc=c), dev(xx=xm, cc=other), dev(cc=other)]
    greet += [dev(yy=lax.rem(y + k, NY)) for k in range(1, NY)]
    greet += [dev(zz=lax.rem(z + k, NZ)) for k in range(1, NZ)]
    for to in greet:
        pl.semaphore_signal(barrier, inc=1, device_id=to, device_id_type=MESH)
    pl.semaphore_wait(barrier, len(greet))

    x_own = c == half_x
    x_odd = 1 - par_x
    x_rel = lax.rem(2 * c + x_odd - x + NX, NX)
    mine = xg.at[par_x, c]
    to_p = rcopy(x_hbm.at[0], mine, "xd", 0, c, dev(xx=xp, cc=half_x))
    to_m = rcopy(x_hbm.at[0], mine, "xd", 1, c, dev(xx=xm, cc=half_x))
    to_p.start()
    to_m.start()
    own_in = pltpu.make_async_copy(x_hbm.at[0], mine, ls.at[4])
    to_other = rcopy(x_hbm.at[0], mine, "xp", 0, 0, dev(cc=other))

    @pl.when(x_own)
    def _():
        own_in.start()

    @pl.when(jnp.logical_not(x_own))
    def _():
        to_other.start()

    upper = (
        lax.broadcasted_iota(jnp.int32, (T, T), 0) <= lax.broadcasted_iota(jnp.int32, (T, T), 1)
    ).astype(F32).astype(BF)
    cumr[...] = jnp.zeros_like(cumr)
    cumr[0:H, :] = ld_ref[0]
    rest = cumr[...]
    total = jnp.zeros((E, T), F32)
    for _ in range(3):
        part = rest.astype(BF)
        total = total + dot(part, upper, 1, 0)
        rest = rest - part.astype(F32)
    cumr[...] = total
    cumc[...] = total.T
    dzs[...] = jnp.broadcast_to(cumr[0:8, T - 1 : T], (8, E))
    dzr[pl.ds(z, 1)] = dzs[...][None]
    sent_dz = []
    for k in range(1, NZ):
        copy = rcopy(dzs, dzr.at[z], "dz", k, k, dev(zz=lax.rem(z + k, NZ)))
        copy.start()
        sent_dz.append(copy)

    lane = lax.broadcasted_iota(jnp.int32, (T, E), 1)

    def column(h):
        return jnp.sum(jnp.where(lane == h, cumc[...], 0.0), axis=1, keepdims=True)

    def cols(h):
        return pl.ds(pl.multiple_of(h * E, E), E)

    loads[0].wait()
    loads[1].wait()

    def term_of(h, carry):
        scaled = gv[:, cols(h)].astype(F32) * jnp.exp(column(h))
        high = scaled.astype(BF)
        low = (scaled - high.astype(F32)).astype(BF)
        query = qv[:, cols(h)].astype(F32).astype(BF)
        term = dot(query, high, 0, 0) + dot(query, low, 0, 0)
        tsend[:, h] = term.astype(BF).reshape(NZ, SL, E)
        return carry

    lax.fori_loop(0, H, term_of, 0)
    trecv[pl.ds(z, 1)] = tsend[pl.ds(z, 1)]
    sent_a1 = []
    for k in range(1, NZ):
        to = lax.rem(z + k, NZ)
        copy = rcopy(tsend.at[to], trecv.at[z], "a1", k, k, dev(zz=to))
        copy.start()
        sent_a1.append(copy)

    loads[2].wait()

    def local_of(h, carry):
        query = qv[:, cols(h)].astype(F32).astype(BF)
        row = cumr[pl.ds(h, 1), :]
        col = column(h)
        for b in range(T // E):
            keys = kv[b * E : (b + 1) * E, cols(h)].astype(F32).astype(BF)
            width = T - b * E
            scores = dot(keys, query[b * E :, :], 1, 1)
            at = lax.broadcasted_iota(jnp.int32, (E, width), 0)
            tok = lax.broadcasted_iota(jnp.int32, (E, width), 1)
            gaps = jnp.where(tok >= at, row[:, b * E :] - col[b * E : (b + 1) * E, :], -jnp.inf)
            weighted = (scores * jnp.exp(gaps)).astype(BF)
            loc[b * E : (b + 1) * E, cols(h)] = dot(weighted, gv[b * E :, cols(h)], 1, 0)
        return carry

    lax.fori_loop(0, H, local_of, 0)

    for k in range(1, NZ):
        src = lax.rem(z + NZ - k, NZ)
        rcopy(dzs, dzr.at[src], "dz", k, k, dev()).wait_recv()
    for k in range(1, NZ):
        src = lax.rem(z + NZ - k, NZ)
        rcopy(tsend.at[0], trecv.at[src], "a1", k, k, dev()).wait_recv()
    logs = [dzr[i] for i in range(NZ)]
    decays = [jnp.exp(v) for v in logs]
    for h in range(H):
        state = jnp.zeros((SL, E), F32)
        for i in range(NZ - 1, -1, -1):
            lbuf[i, h] = state
            state = trecv[i, h].astype(F32) + decays[i][h : h + 1, :] * state
        ysend[h * SL : (h + 1) * SL, :] = state
    later = [jnp.zeros((8, E), F32)]
    for i in range(NZ - 1, -1, -1):
        later.append(later[-1] + logs[i])
    ysend[H * SL :, :] = later[NZ]
    yrecv[pl.ds(y, 1)] = ysend[...][None]
    sent_yx = []
    for k in range(1, NY):
        copy = rcopy(ysend, yrecv.at[y], "yx", k, k, dev(yy=lax.rem(y + k, NY)))
        copy.start()
        sent_yx.append(copy)
    for k in range(1, NY):
        src = lax.rem(y + NY - k, NY)
        rcopy(ysend, yrecv.at[src], "yx", k, k, dev()).wait_recv()
    y_decay = [jnp.exp(yrecv[j, H * SL :, :]) for j in range(NY)]
    z_decay = [jnp.exp(later[NZ - 1 - i]) for i in range(NZ)]
    for h in range(H):
        state = jnp.zeros((SL, E), F32)
        for j in range(NY - 1, 0, -1):
            new = yrecv[j, h * SL : (h + 1) * SL, :] + y_decay[j][h : h + 1, :] * state
            state = jnp.where(y < j, new, state)
        for i in range(NZ):
            csend[i, h] = (lbuf[i, h] + z_decay[i][h : h + 1, :] * state).astype(BF)
    crecv[pl.ds(z, 1)] = csend[pl.ds(z, 1)]
    sent_a2 = []
    for k in range(1, NZ):
        to = lax.rem(z + k, NZ)
        copy = rcopy(csend.at[to], crecv.at[z], "a2", k, k, dev(zz=to))
        copy.start()
        sent_a2.append(copy)

    for i in range(2):
        rcopy(x_hbm.at[0], xg.at[x_odd, i], "xd", 0, i, dev()).wait_recv()
    rows_a, rows_b = pl.ds(0, HT), pl.ds(HT, HT)
    half_a, half_b = xg.at[x_odd, :, rows_a, :], xg.at[x_odd, :, rows_b, :]
    pass_a = rcopy(half_a, half_a, "xf", 0, 0, dev(xx=xm))
    pass_b = rcopy(half_b, half_b, "xf", 1, 1, dev(xx=xp))

    @pl.when(x_rel == 1)
    def _():
        pass_a.start()

    @pl.when(x_rel == 3)
    def _():
        pass_b.start()

    for k in range(1, NZ):
        src = lax.rem(z + NZ - k, NZ)
        rcopy(csend.at[0], crecv.at[src], "a2", k, k, dev()).wait_recv()

    def value_of(h, carry):
        col = column(h)
        keys = kv[:, cols(h)].astype(F32).astype(BF)
        carried = jnp.exp(col[T - 1 : T, :] - col) * dot(keys, crecv[:, h].reshape(E, E), 1, 0)
        vgs[c, :, cols(h)] = (grad_scale * (loc[:, cols(h)] + carried)).astype(BF)
        return carry

    lax.fori_loop(0, H, value_of, 0)
    sent_vg = rcopy(vgs.at[c], vgs.at[c], "vg", 0, 0, dev(cc=other))
    sent_vg.start()

    loads[3].wait()

    def product(to):
        block = wv[pl.ds(pl.multiple_of(to * F, F), F), :]
        return dot(vgs[c], block, 1, 1)

    p2s[...] = product(lax.rem(x + 2, NX)).astype(BF)
    sent_x = [
        rcopy(p2s.at[rows_a], xh.at[0], "xh", 0, 0, dev(xx=xp)),
        rcopy(p2s.at[rows_b], xh.at[1], "xh", 1, 1, dev(xx=xm)),
    ]
    for copy in sent_x:
        copy.start()
    near = product(xp)
    pf[0] = near[:HT]
    pss[0, HT:, :] = near[HT:].astype(BF)
    copy = rcopy(pss.at[0, rows_b], xf.at[0, rows_b], "xs", 0, 0, dev(xx=xp))
    copy.start()
    sent_x.append(copy)
    near = product(xm)
    pf[1] = near[HT:]
    pss[1, :HT, :] = near[:HT].astype(BF)
    copy = rcopy(pss.at[1, rows_a], xf.at[1, rows_a], "xs", 1, 1, dev(xx=xm))
    copy.start()
    sent_x.append(copy)

    y_own = c == half_y
    y_odd = 1 - par_y
    y_rel = lax.rem(2 * c + y_odd - y + NY, NY)

    @pl.when(x_own)
    def _():
        own_in.wait()
        rcopy(x_hbm.at[0], xg.at[par_x, other], "xp", 0, 0, dev()).wait_recv()

    @pl.when(jnp.logical_not(x_own))
    def _():
        far_a, far_b = xg.at[par_x, :, rows_a, :], xg.at[par_x, :, rows_b, :]
        rcopy(far_a, far_a, "xf", 0, 0, dev()).wait_recv()
        rcopy(far_b, far_b, "xf", 1, 1, dev()).wait_recv()

    rcopy(vgs.at[other], vgs.at[other], "vg", 0, 0, dev()).wait_recv()

    def weight_of(i, carry):
        slot = lax.rem(par_y + jnp.where(y_own, 1, 0) + i, 2)
        dwf[slot] = dot(xg[slot].reshape(2 * T, F), vgs[...].reshape(2 * T, F), 0, 0)
        dsend[slot] = dwf[slot].astype(BF)
        first_a, first_b = pl.ds(0, HF), pl.ds(HF, HF)

        @pl.when(jnp.logical_and(slot == par_y, jnp.logical_not(y_own)))
        def _():
            rcopy(dsend.at[slot, first_a], yh, "yh", 0, 0, dev(yy=yp)).start()
            rcopy(dsend.at[slot, first_b], yh, "yh", 1, 0, dev(yy=ym)).start()

        @pl.when(jnp.logical_and(slot == y_odd, y_rel == 1))
        def _():
            rcopy(dsend.at[slot, first_b], yf.at[0, first_b], "ys", 1, 1, dev(yy=yp)).start()

        @pl.when(jnp.logical_and(slot == y_odd, y_rel == 3))
        def _():
            rcopy(dsend.at[slot, first_a], yf.at[1, first_a], "ys", 2, 2, dev(yy=ym)).start()

        return carry

    lax.fori_loop(0, 2, weight_of, 0)

    rcopy(p2s.at[rows_a], xh.at[0], "xh", 0, 0, dev()).wait_recv()
    pss[0, :HT, :] = (pf[0] + xh[0].astype(F32)).astype(BF)
    copy = rcopy(pss.at[0, rows_a], xf.at[0, rows_a], "xs", 2, 2, dev(xx=xp))
    copy.start()
    sent_x.append(copy)
    rcopy(p2s.at[rows_b], xh.at[1], "xh", 1, 1, dev()).wait_recv()
    pss[1, HT:, :] = (pf[1] + xh[1].astype(F32)).astype(BF)
    copy = rcopy(pss.at[1, rows_b], xf.at[1, rows_b], "xs", 3, 3, dev(xx=xm))
    copy.start()
    sent_x.append(copy)
    loc[...] = product(x)

    rows_a4, rows_b4 = pl.ds(0, HF), pl.ds(HF, HF)
    rcopy(dsend.at[0, rows_a4], yh, "yh", 0, 0, dev()).wait_recv()

    @pl.when(y_rel == 1)
    def _():
        dsend[y_odd, 0:HF, :] = (dwf[y_odd, 0:HF, :] + yh[...].astype(F32)).astype(BF)
        rcopy(dsend.at[y_odd, rows_a4], yf.at[0, rows_a4], "ys", 0, 0, dev(yy=yp)).start()

    @pl.when(y_rel == 3)
    def _():
        dsend[y_odd, HF:F, :] = (dwf[y_odd, HF:F, :] + yh[...].astype(F32)).astype(BF)
        rcopy(dsend.at[y_odd, rows_b4], yf.at[1, rows_b4], "ys", 3, 3, dev(yy=ym)).start()

    rcopy(pss.at[0, rows_b], xf.at[0, rows_b], "xs", 0, 0, dev()).wait_recv()
    rcopy(pss.at[0, rows_a], xf.at[0, rows_a], "xs", 2, 2, dev()).wait_recv()
    rcopy(pss.at[1, rows_a], xf.at[1, rows_a], "xs", 1, 1, dev()).wait_recv()
    rcopy(pss.at[1, rows_b], xf.at[1, rows_b], "xs", 3, 3, dev()).wait_recv()
    gio[...] = (loc[...] + xf[0].astype(F32) + xf[1].astype(F32)).astype(BF)
    out_gi = pltpu.make_async_copy(gio, gi_hbm.at[0], ls.at[5])
    out_gi.start()

    @pl.when(y_own)
    def _():
        for i, rows in ((0, rows_a4), (1, rows_b4)):
            for side in range(2):
                rcopy(
                    dsend.at[0, rows], yf.at[side, rows], "ys", 2 * side + i, 2 * side + i, dev()
                ).wait_recv()
        dwf[par_y] = dwf[par_y] + yf[0].astype(F32) + yf[1].astype(F32)

        def rows_for(to):
            return pl.ds(pl.multiple_of(to * ZR, 16), ZR)

        started = []

        def hop(name, send, got, step, to, n, way, cut):
            at, width = CUTS[cut]
            span = pl.ds(at, width)
            value = dwf[par_y, rows_for(to), span]
            if step > 0:
                idx = 2 * (step - 1) + cut
                rcopy(send.at[step - 1, :, span], got.at[step - 1, :, span], name, idx, idx, dev()).wait_recv()
                value = value + got[step - 1, :, span].astype(F32)
            if step == n:
                return value
            send[step, :, span] = value.astype(BF)
            idx = 2 * step + cut
            copy = rcopy(send.at[step, :, span], got.at[step, :, span], name, idx, idx, dev(zz=way))
            copy.start()
            started.append(copy)

        for step in range(4):
            for cut in range(2):
                hop("zp", zps, zpr, step, lax.rem(z + 4 - step, NZ), 4, zp, cut)
                if step < 3:
                    hop("zm", zms, zmr, step, lax.rem(z + 5 + step, NZ), 3, zm, cut)
        for cut in range(2):
            at, width = CUTS[cut]
            span = pl.ds(at, width)
            value = hop("zp", zps, zpr, 4, z, 4, zp, cut)
            idx = 4 + cut
            rcopy(zms.at[2, :, span], zmr.at[2, :, span], "zm", idx, idx, dev()).wait_recv()
            fin[:, span] = weight_scale * (value + zmr[2, :, span].astype(F32))
        keep = pl.ds(pl.multiple_of(c * OUT, 8), OUT)
        give = pl.ds(pl.multiple_of(other * OUT, 8), OUT)
        copy = rcopy(fin.at[give], gwv, "fp", 0, 0, dev(cc=other))
        copy.start()
        started.append(copy)
        out = pltpu.make_async_copy(fin.at[keep], gw_hbm, ls.at[6])
        out.start()
        for copy in started:
            copy.wait_send()
        out.wait()

    @pl.when(jnp.logical_not(y_own))
    def _():
        rcopy(fin.at[pl.ds(0, OUT)], gwv, "fp", 0, 0, dev()).wait_recv()
        out = pltpu.make_async_copy(gwv, gw_hbm, ls.at[6])
        out.start()
        rcopy(dsend.at[par_y, rows_a4], yh, "yh", 0, 0, dev()).wait_send()
        rcopy(dsend.at[par_y, rows_b4], yh, "yh", 1, 0, dev()).wait_send()
        out.wait()

    out_gi.wait()
    to_p.wait_send()
    to_m.wait_send()

    @pl.when(jnp.logical_not(x_own))
    def _():
        to_other.wait_send()

    @pl.when(x_rel == 1)
    def _():
        pass_a.wait_send()

    @pl.when(x_rel == 3)
    def _():
        pass_b.wait_send()

    @pl.when(y_rel == 1)
    def _():
        rcopy(dsend.at[y_odd, rows_a4], yf.at[0, rows_a4], "ys", 0, 0, dev()).wait_send()
        rcopy(dsend.at[y_odd, rows_b4], yf.at[0, rows_b4], "ys", 1, 1, dev()).wait_send()

    @pl.when(y_rel == 3)
    def _():
        rcopy(dsend.at[y_odd, rows_a4], yf.at[1, rows_a4], "ys", 2, 2, dev()).wait_send()
        rcopy(dsend.at[y_odd, rows_b4], yf.at[1, rows_b4], "ys", 3, 3, dev()).wait_send()

    for copy in sent_dz + sent_a1 + sent_yx + sent_a2 + [sent_vg] + sent_x:
        copy.wait_send()


def local(inputs, value_weight, cotangent, spikes_q, spikes_k, log_decay):
    grad_scale = 1.0 / (2.25 * E * math.sqrt(T * NY * NZ))
    weight_scale = 1.0 / math.sqrt(2 * T * NY * NZ)
    vm = pltpu.VMEM
    anywhere = pl.BlockSpec(memory_space=pl.ANY)

    def body(*refs):
        kernel(grad_scale, weight_scale, *refs)

    return pl.pallas_call(
        body,
        out_shape=(
            jax.ShapeDtypeStruct((1, T, F), BF),
            jax.ShapeDtypeStruct((OUT, F), F32),
        ),
        in_specs=[anywhere] * 5 + [pl.BlockSpec(memory_space=pltpu.VMEM)],
        out_specs=(anywhere, anywhere),
        scratch_shapes=[
            vm((NX * F, F), BF),
            vm((T, F), BF),
            vm((T, F), jnp.int32),
            vm((T, F), jnp.int32),
            vm((2, 2, T, F), BF),
            vm((E, T), F32),
            vm((T, E), F32),
            vm((8, E), F32),
            vm((NZ, 8, E), F32),
            vm((NZ, H, SL, E), BF),
            vm((NZ, H, SL, E), BF),
            vm((NZ, H, SL, E), F32),
            vm((YROWS, E), F32),
            vm((NY, YROWS, E), F32),
            vm((NZ, H, SL, E), BF),
            vm((NZ, H, SL, E), BF),
            vm((T, F), F32),
            vm((2, T, F), BF),
            vm((T, F), BF),
            vm((2, T, F), BF),
            vm((2, HT, F), F32),
            vm((2, HT, F), BF),
            vm((2, T, F), BF),
            vm((T, F), BF),
            vm((2, F, F), F32),
            vm((2, F, F), BF),
            vm((HF, F), BF),
            vm((2, F, F), BF),
            vm((4, ZR, F), BF),
            vm((4, ZR, F), BF),
            vm((3, ZR, F), BF),
            vm((3, ZR, F), BF),
            vm((ZR, F), F32),
            vm((OUT, F), F32),
            pltpu.SemaphoreType.DMA((NSEM,)),
            pltpu.SemaphoreType.DMA((NSEM,)),
            pltpu.SemaphoreType.DMA((7,)),
        ],
        compiler_params=pltpu.CompilerParams(
            collective_id=0, has_side_effects=True, vmem_limit_bytes=60 * 1024 * 1024
        ),
    )(inputs, value_weight, cotangent, spikes_q, spikes_k, log_decay)


def solution(mesh):
    return jax.shard_map(
        local,
        mesh=mesh,
        in_specs=(
            P("dp", "seq", "head"),
            P(None, "head"),
            P("dp", "seq", "head"),
            P("dp", "seq", "head"),
            P("dp", "seq", "head"),
            P("dp", "head", "seq"),
        ),
        out_specs=(P("dp", "seq", "head"), P(("seq", "dp"), "head")),
        check_vma=False,
    )
```

```python
import math

import jax
import jax.numpy as jnp
from jax import lax
from jax.experimental import pallas as pl
from jax.experimental.pallas import tpu as pltpu
from jax.sharding import PartitionSpec as P

NX, NY, NZ = 4, 4, 8
T, F, H, E = 512, 896, 7, 128
HT = T // 2
HF = F // 2
ZR = F // NZ
OUT = ZR // 2
SL = E // NZ
YROWS = H * SL + 8
CUTS = ((0, 384), (384, 256), (640, 256))
NC = len(CUTS)
BF, F32 = jnp.bfloat16, jnp.float32
MESH = pl.DeviceIdType.MESH

_names = {}
_count = 0
for _name, _n in (
    ("dz", 8), ("a1", 8), ("a2", 8), ("yx", 4), ("xd", 2), ("xp", 1), ("xf", 2), ("vg", 1),
    ("xh", 2), ("xs", 4), ("yh", 2 * NC), ("ys", 4 * NC), ("zp", 4 * NC), ("zm", 3 * NC), ("fp", 1),
):
    _names[_name] = _count
    _count += _n
NSEM = _count


def dot(a, b, ca, cb):
    return lax.dot_general(a, b, (((ca,), (cb,)), ((), ())), preferred_element_type=F32)


def kernel(
    grad_scale, weight_scale,
    x_hbm, w_hbm, g_hbm, q_hbm, k_hbm, ld_hbm,
    gi_hbm, gw_hbm,
    ldv, wv, gv, qv, kv, xg, cumr, cumc, dzs, dzr, tsend, trecv, lbuf, ysend, yrecv, csend, crecv,
    loc, vgs, p2s, pss, pf, xh, xf, gio, dwf, dsend, yh, yf, zps, zpr, zms, zmr, fin, gwv,
    ss, rs, ls,
):
    s = lax.axis_index("seq")
    x = lax.axis_index("head")
    c = lax.axis_index("dp")
    y, z = lax.div(s, NZ), lax.rem(s, NZ)
    half_x, par_x = lax.div(x, 2), lax.rem(x, 2)
    half_y, par_y = lax.div(y, 2), lax.rem(y, 2)
    other = 1 - c
    xp, xm = lax.rem(x + 1, NX), lax.rem(x + NX - 1, NX)
    yp, ym = lax.rem(y + 1, NY), lax.rem(y + NY - 1, NY)
    zp, zm = lax.rem(z + 1, NZ), lax.rem(z + NZ - 1, NZ)

    def dev(yy=None, zz=None, xx=None, cc=None):
        yy = y if yy is None else yy
        zz = z if zz is None else zz
        return (yy * NZ + zz, x if xx is None else xx, c if cc is None else cc)

    def rcopy(src, dst, name, send, recv, to):
        base = _names[name]
        return pltpu.make_async_remote_copy(
            src_ref=src, dst_ref=dst, send_sem=ss.at[base + send], recv_sem=rs.at[base + recv],
            device_id=to, device_id_type=MESH,
        )

    loads = [
        pltpu.make_async_copy(q_hbm.at[0], qv, ls.at[0]),
        pltpu.make_async_copy(g_hbm.at[0], gv, ls.at[1]),
        pltpu.make_async_copy(k_hbm.at[0], kv, ls.at[2]),
        pltpu.make_async_copy(w_hbm, wv, ls.at[3]),
        pltpu.make_async_copy(ld_hbm, ldv, ls.at[7]),
    ]
    for load in loads:
        load.start()

    barrier = pltpu.get_barrier_semaphore()
    greet = [dev(xx=xp, cc=c), dev(xx=xp, cc=other), dev(xx=xm, cc=c), dev(xx=xm, cc=other), dev(cc=other)]
    greet += [dev(yy=lax.rem(y + k, NY)) for k in range(1, NY)]
    greet += [dev(zz=lax.rem(z + k, NZ)) for k in range(1, NZ)]
    for to in greet:
        pl.semaphore_signal(barrier, inc=1, device_id=to, device_id_type=MESH)
    pl.semaphore_wait(barrier, len(greet))

    x_own = c == half_x
    x_odd = 1 - par_x
    x_rel = lax.rem(2 * c + x_odd - x + NX, NX)
    mine = xg.at[par_x, c]
    to_p = rcopy(x_hbm.at[0], mine, "xd", 0, c, dev(xx=xp, cc=half_x))
    to_m = rcopy(x_hbm.at[0], mine, "xd", 1, c, dev(xx=xm, cc=half_x))
    to_p.start()
    to_m.start()
    own_in = pltpu.make_async_copy(x_hbm.at[0], mine, ls.at[4])
    to_other = rcopy(x_hbm.at[0], mine, "xp", 0, 0, dev(cc=other))

    @pl.when(x_own)
    def _():
        own_in.start()

    @pl.when(jnp.logical_not(x_own))
    def _():
        to_other.start()

    upper = (
        lax.broadcasted_iota(jnp.int32, (T, T), 0) <= lax.broadcasted_iota(jnp.int32, (T, T), 1)
    ).astype(F32).astype(BF)
    cumr[...] = jnp.zeros_like(cumr)
    loads[4].wait()
    cumr[0:H, :] = ldv[0]
    rest = cumr[...]
    total = jnp.zeros((E, T), F32)
    for _ in range(3):
        part = rest.astype(BF)
        total = total + dot(part, upper, 1, 0)
        rest = rest - part.astype(F32)
    cumr[...] = total
    cumc[...] = total.T
    dzs[...] = jnp.broadcast_to(cumr[0:8, T - 1 : T], (8, E))
    dzr[pl.ds(z, 1)] = dzs[...][None]
    sent_dz = []
    for k in range(1, NZ):
        copy = rcopy(dzs, dzr.at[z], "dz", k, k, dev(zz=lax.rem(z + k, NZ)))
        copy.start()
        sent_dz.append(copy)

    lane = lax.broadcasted_iota(jnp.int32, (T, E), 1)

    def column(h):
        return jnp.sum(jnp.where(lane == h, cumc[...], 0.0), axis=1, keepdims=True)

    def cols(h):
        return pl.ds(pl.multiple_of(h * E, E), E)

    loads[0].wait()
    loads[1].wait()

    def term_of(h, carry):
        scaled = gv[:, cols(h)].astype(F32) * jnp.exp(column(h))
        high = scaled.astype(BF)
        low = (scaled - high.astype(F32)).astype(BF)
        query = qv[:, cols(h)].astype(F32).astype(BF)
        term = dot(query, high, 0, 0) + dot(query, low, 0, 0)
        tsend[:, h] = term.astype(BF).reshape(NZ, SL, E)
        return carry

    lax.fori_loop(0, H, term_of, 0)
    trecv[pl.ds(z, 1)] = tsend[pl.ds(z, 1)]
    sent_a1 = []
    for k in range(1, NZ):
        to = lax.rem(z + k, NZ)
        copy = rcopy(tsend.at[to], trecv.at[z], "a1", k, k, dev(zz=to))
        copy.start()
        sent_a1.append(copy)

    loads[2].wait()

    def local_of(h, carry):
        query = qv[:, cols(h)].astype(F32).astype(BF)
        row = cumr[pl.ds(h, 1), :]
        col = column(h)
        for b in range(T // E):
            keys = kv[b * E : (b + 1) * E, cols(h)].astype(F32).astype(BF)
            width = T - b * E
            scores = dot(keys, query[b * E :, :], 1, 1)
            at = lax.broadcasted_iota(jnp.int32, (E, width), 0)
            tok = lax.broadcasted_iota(jnp.int32, (E, width), 1)
            gaps = jnp.where(tok >= at, row[:, b * E :] - col[b * E : (b + 1) * E, :], -jnp.inf)
            weighted = (scores * jnp.exp(gaps)).astype(BF)
            loc[b * E : (b + 1) * E, cols(h)] = dot(weighted, gv[b * E :, cols(h)], 1, 0)
        return carry

    lax.fori_loop(0, H, local_of, 0)

    for k in range(1, NZ):
        src = lax.rem(z + NZ - k, NZ)
        rcopy(dzs, dzr.at[src], "dz", k, k, dev()).wait_recv()
    for k in range(1, NZ):
        src = lax.rem(z + NZ - k, NZ)
        rcopy(tsend.at[0], trecv.at[src], "a1", k, k, dev()).wait_recv()
    logs = [dzr[i] for i in range(NZ)]
    decays = [jnp.exp(v) for v in logs]
    for h in range(H):
        state = jnp.zeros((SL, E), F32)
        for i in range(NZ - 1, -1, -1):
            lbuf[i, h] = state
            state = trecv[i, h].astype(F32) + decays[i][h : h + 1, :] * state
        ysend[h * SL : (h + 1) * SL, :] = state
    later = [jnp.zeros((8, E), F32)]
    for i in range(NZ - 1, -1, -1):
        later.append(later[-1] + logs[i])
    ysend[H * SL :, :] = later[NZ]
    yrecv[pl.ds(y, 1)] = ysend[...][None]
    sent_yx = []
    for k in range(1, NY):
        copy = rcopy(ysend, yrecv.at[y], "yx", k, k, dev(yy=lax.rem(y + k, NY)))
        copy.start()
        sent_yx.append(copy)
    for k in range(1, NY):
        src = lax.rem(y + NY - k, NY)
        rcopy(ysend, yrecv.at[src], "yx", k, k, dev()).wait_recv()
    y_decay = [jnp.exp(yrecv[j, H * SL :, :]) for j in range(NY)]
    z_decay = [jnp.exp(later[NZ - 1 - i]) for i in range(NZ)]
    for h in range(H):
        state = jnp.zeros((SL, E), F32)
        for j in range(NY - 1, 0, -1):
            new = yrecv[j, h * SL : (h + 1) * SL, :] + y_decay[j][h : h + 1, :] * state
            state = jnp.where(y < j, new, state)
        for i in range(NZ):
            csend[i, h] = (lbuf[i, h] + z_decay[i][h : h + 1, :] * state).astype(BF)
    crecv[pl.ds(z, 1)] = csend[pl.ds(z, 1)]
    sent_a2 = []
    for k in range(1, NZ):
        to = lax.rem(z + k, NZ)
        copy = rcopy(csend.at[to], crecv.at[z], "a2", k, k, dev(zz=to))
        copy.start()
        sent_a2.append(copy)

    for i in range(2):
        rcopy(x_hbm.at[0], xg.at[x_odd, i], "xd", 0, i, dev()).wait_recv()
    rows_a, rows_b = pl.ds(0, HT), pl.ds(HT, HT)
    half_a, half_b = xg.at[x_odd, :, rows_a, :], xg.at[x_odd, :, rows_b, :]
    pass_a = rcopy(half_a, half_a, "xf", 0, 0, dev(xx=xm))
    pass_b = rcopy(half_b, half_b, "xf", 1, 1, dev(xx=xp))

    @pl.when(x_rel == 1)
    def _():
        pass_a.start()

    @pl.when(x_rel == 3)
    def _():
        pass_b.start()

    for k in range(1, NZ):
        src = lax.rem(z + NZ - k, NZ)
        rcopy(csend.at[0], crecv.at[src], "a2", k, k, dev()).wait_recv()

    def value_of(h, carry):
        col = column(h)
        keys = kv[:, cols(h)].astype(F32).astype(BF)
        carried = jnp.exp(col[T - 1 : T, :] - col) * dot(keys, crecv[:, h].reshape(E, E), 1, 0)
        vgs[c, :, cols(h)] = (grad_scale * (loc[:, cols(h)] + carried)).astype(BF)
        return carry

    lax.fori_loop(0, H, value_of, 0)
    sent_vg = rcopy(vgs.at[c], vgs.at[c], "vg", 0, 0, dev(cc=other))
    sent_vg.start()

    loads[3].wait()

    def product(to):
        block = wv[pl.ds(pl.multiple_of(to * F, F), F), :]
        return dot(vgs[c], block, 1, 1)

    p2s[...] = product(lax.rem(x + 2, NX)).astype(BF)
    sent_x = [
        rcopy(p2s.at[rows_a], xh.at[0], "xh", 0, 0, dev(xx=xp)),
        rcopy(p2s.at[rows_b], xh.at[1], "xh", 1, 1, dev(xx=xm)),
    ]
    for copy in sent_x:
        copy.start()
    near = product(xp)
    pf[0] = near[:HT]
    pss[0, HT:, :] = near[HT:].astype(BF)
    copy = rcopy(pss.at[0, rows_b], xf.at[0, rows_b], "xs", 0, 0, dev(xx=xp))
    copy.start()
    sent_x.append(copy)
    near = product(xm)
    pf[1] = near[HT:]
    pss[1, :HT, :] = near[:HT].astype(BF)
    copy = rcopy(pss.at[1, rows_a], xf.at[1, rows_a], "xs", 1, 1, dev(xx=xm))
    copy.start()
    sent_x.append(copy)

    y_own = c == half_y
    y_odd = 1 - par_y
    y_rel = lax.rem(2 * c + y_odd - y + NY, NY)

    rcopy(vgs.at[other], vgs.at[other], "vg", 0, 0, dev()).wait_recv()
    rows_a4, rows_b4 = pl.ds(0, HF), pl.ds(HF, HF)
    spans = [pl.ds(at, width) for at, width in CUTS]

    def to_near(slot, cut):
        half = rows_a4, rows_b4
        return [
            rcopy(dsend.at[slot, half[i], spans[cut]], yh.at[:, spans[cut]], "yh", i * NC + cut, cut,
                  dev(yy=(yp, ym)[i]))
            for i in range(2)
        ]

    def to_owner(slot, side, half, cut):
        rows = (rows_a4, rows_b4)[half]
        idx = (2 * side + half) * NC + cut
        return rcopy(
            dsend.at[slot, rows, spans[cut]], yf.at[side, rows, spans[cut]], "ys", idx, idx,
            dev(yy=(yp, ym)[side]),
        )

    def weight_of(i, carry):
        slot = lax.rem(par_x + jnp.where(x_own, 0, 1) + i, 2)

        @pl.when(jnp.logical_and(slot == par_x, x_own))
        def _():
            own_in.wait()
            rcopy(x_hbm.at[0], xg.at[par_x, other], "xp", 0, 0, dev()).wait_recv()

        @pl.when(jnp.logical_and(slot == par_x, jnp.logical_not(x_own)))
        def _():
            far_a, far_b = xg.at[par_x, :, rows_a, :], xg.at[par_x, :, rows_b, :]
            rcopy(far_a, far_a, "xf", 0, 0, dev()).wait_recv()
            rcopy(far_b, far_b, "xf", 1, 1, dev()).wait_recv()

        dwf[slot] = dot(xg[slot].reshape(2 * T, F), vgs[...].reshape(2 * T, F), 0, 0)
        dsend[slot] = dwf[slot].astype(BF)

        @pl.when(jnp.logical_and(slot == par_y, jnp.logical_not(y_own)))
        def _():
            for cut in range(NC):
                for copy in to_near(slot, cut):
                    copy.start()

        @pl.when(jnp.logical_and(slot == y_odd, y_rel == 1))
        def _():
            for cut in range(NC):
                to_owner(slot, 0, 1, cut).start()

        @pl.when(jnp.logical_and(slot == y_odd, y_rel == 3))
        def _():
            for cut in range(NC):
                to_owner(slot, 1, 0, cut).start()

        return carry

    lax.fori_loop(0, 2, weight_of, 0)
    loc[...] = product(x)

    for cut in range(NC):
        span = spans[cut]
        rcopy(dsend.at[0, rows_a4, span], yh.at[:, span], "yh", cut, cut, dev()).wait_recv()

        @pl.when(y_rel == 1)
        def _():
            dsend[y_odd, 0:HF, span] = (dwf[y_odd, 0:HF, span] + yh[:, span].astype(F32)).astype(BF)
            to_owner(y_odd, 0, 0, cut).start()

        @pl.when(y_rel == 3)
        def _():
            dsend[y_odd, HF:F, span] = (dwf[y_odd, HF:F, span] + yh[:, span].astype(F32)).astype(BF)
            to_owner(y_odd, 1, 1, cut).start()

    rcopy(p2s.at[rows_a], xh.at[0], "xh", 0, 0, dev()).wait_recv()
    pss[0, :HT, :] = (pf[0] + xh[0].astype(F32)).astype(BF)
    copy = rcopy(pss.at[0, rows_a], xf.at[0, rows_a], "xs", 2, 2, dev(xx=xp))
    copy.start()
    sent_x.append(copy)
    rcopy(p2s.at[rows_b], xh.at[1], "xh", 1, 1, dev()).wait_recv()
    pss[1, HT:, :] = (pf[1] + xh[1].astype(F32)).astype(BF)
    copy = rcopy(pss.at[1, rows_b], xf.at[1, rows_b], "xs", 3, 3, dev(xx=xm))
    copy.start()
    sent_x.append(copy)

    keep = pl.ds(pl.multiple_of(c * OUT, 8), OUT)
    give = pl.ds(pl.multiple_of(other * OUT, 8), OUT)
    out_fin = pltpu.make_async_copy(fin.at[keep], gw_hbm, ls.at[6])
    give_fin = rcopy(fin.at[give], gwv, "fp", 0, 0, dev(cc=other))

    def along_z(name, step, cut):
        send, got, way = (zps, zpr, zp) if name == "zp" else (zms, zmr, zm)
        idx = step * NC + cut
        part = (step, slice(None), spans[cut])
        return rcopy(send.at[part], got.at[part], name, idx, idx, dev(zz=way))

    def hop(name, step, to, cut, last):
        send, got = (zps, zpr) if name == "zp" else (zms, zmr)
        span = spans[cut]
        value = dwf[par_y, pl.ds(pl.multiple_of(to * ZR, 16), ZR), span]
        if step > 0:
            along_z(name, step - 1, cut).wait_recv()
            value = value + got[step - 1, :, span].astype(F32)
        if step == last:
            return value
        send[step, :, span] = value.astype(BF)
        along_z(name, step, cut).start()

    @pl.when(y_own)
    def _():
        for tick in range(4 + NC):
            for cut in range(NC):
                step, span = tick - cut, spans[cut]
                if step < 0 or step > 4:
                    continue
                if step == 0:
                    for side in range(2):
                        for half in range(2):
                            to_owner(0, side, half, cut).wait_recv()
                    dwf[par_y, :, span] = (
                        dwf[par_y, :, span] + yf[0, :, span].astype(F32) + yf[1, :, span].astype(F32)
                    )
                value = hop("zp", step, lax.rem(z + 4 - step + NZ, NZ), cut, 4)
                if step < 3:
                    hop("zm", step, lax.rem(z + 5 + step, NZ), cut, 3)
                if step == 4:
                    along_z("zm", 2, cut).wait_recv()
                    fin[:, span] = weight_scale * (value + zmr[2, :, span].astype(F32))
        give_fin.start()
        out_fin.start()

    rcopy(pss.at[0, rows_b], xf.at[0, rows_b], "xs", 0, 0, dev()).wait_recv()
    rcopy(pss.at[0, rows_a], xf.at[0, rows_a], "xs", 2, 2, dev()).wait_recv()
    rcopy(pss.at[1, rows_a], xf.at[1, rows_a], "xs", 1, 1, dev()).wait_recv()
    rcopy(pss.at[1, rows_b], xf.at[1, rows_b], "xs", 3, 3, dev()).wait_recv()
    gio[...] = (loc[...] + xf[0].astype(F32) + xf[1].astype(F32)).astype(BF)
    out_gi = pltpu.make_async_copy(gio, gi_hbm.at[0], ls.at[5])
    out_gi.start()

    @pl.when(y_own)
    def _():
        for cut in range(NC):
            for step in range(4):
                along_z("zp", step, cut).wait_send()
            for step in range(3):
                along_z("zm", step, cut).wait_send()
        give_fin.wait_send()
        out_fin.wait()

    @pl.when(jnp.logical_not(y_own))
    def _():
        rcopy(fin.at[pl.ds(0, OUT)], gwv, "fp", 0, 0, dev()).wait_recv()
        out = pltpu.make_async_copy(gwv, gw_hbm, ls.at[6])
        out.start()
        for cut in range(NC):
            for copy in to_near(par_y, cut):
                copy.wait_send()
        out.wait()

    out_gi.wait()
    to_p.wait_send()
    to_m.wait_send()

    @pl.when(jnp.logical_not(x_own))
    def _():
        to_other.wait_send()

    @pl.when(x_rel == 1)
    def _():
        pass_a.wait_send()

    @pl.when(x_rel == 3)
    def _():
        pass_b.wait_send()

    for side in range(2):
        @pl.when(y_rel == 1 + 2 * side)
        def _():
            for half in range(2):
                for cut in range(NC):
                    to_owner(y_odd, side, half, cut).wait_send()

    for copy in sent_dz + sent_a1 + sent_yx + sent_a2 + [sent_vg] + sent_x:
        copy.wait_send()


def local(inputs, value_weight, cotangent, spikes_q, spikes_k, log_decay):
    grad_scale = 1.0 / (2.25 * E * math.sqrt(T * NY * NZ))
    weight_scale = 1.0 / math.sqrt(2 * T * NY * NZ)
    vm = pltpu.VMEM
    anywhere = pl.BlockSpec(memory_space=pl.ANY)

    def body(*refs):
        kernel(grad_scale, weight_scale, *refs)

    return pl.pallas_call(
        body,
        out_shape=(
            jax.ShapeDtypeStruct((1, T, F), BF),
            jax.ShapeDtypeStruct((OUT, F), F32),
        ),
        in_specs=[anywhere] * 6,
        out_specs=(anywhere, anywhere),
        scratch_shapes=[
            vm((1, H, T), F32),
            vm((NX * F, F), BF),
            vm((T, F), BF),
            vm((T, F), jnp.int32),
            vm((T, F), jnp.int32),
            vm((2, 2, T, F), BF),
            vm((E, T), F32),
            vm((T, E), F32),
            vm((8, E), F32),
            vm((NZ, 8, E), F32),
            vm((NZ, H, SL, E), BF),
            vm((NZ, H, SL, E), BF),
            vm((NZ, H, SL, E), F32),
            vm((YROWS, E), F32),
            vm((NY, YROWS, E), F32),
            vm((NZ, H, SL, E), BF),
            vm((NZ, H, SL, E), BF),
            vm((T, F), F32),
            vm((2, T, F), BF),
            vm((T, F), BF),
            vm((2, T, F), BF),
            vm((2, HT, F), F32),
            vm((2, HT, F), BF),
            vm((2, T, F), BF),
            vm((T, F), BF),
            vm((2, F, F), F32),
            vm((2, F, F), BF),
            vm((HF, F), BF),
            vm((2, F, F), BF),
            vm((4, ZR, F), BF),
            vm((4, ZR, F), BF),
            vm((3, ZR, F), BF),
            vm((3, ZR, F), BF),
            vm((ZR, F), F32),
            vm((OUT, F), F32),
            pltpu.SemaphoreType.DMA((NSEM,)),
            pltpu.SemaphoreType.DMA((NSEM,)),
            pltpu.SemaphoreType.DMA((8,)),
        ],
        compiler_params=pltpu.CompilerParams(
            collective_id=0, has_side_effects=True, vmem_limit_bytes=60 * 1024 * 1024
        ),
    )(inputs, value_weight, cotangent, spikes_q, spikes_k, log_decay)


def solution(mesh):
    return jax.shard_map(
        local,
        mesh=mesh,
        in_specs=(
            P("dp", "seq", "head"),
            P(None, "head"),
            P("dp", "seq", "head"),
            P("dp", "seq", "head"),
            P("dp", "seq", "head"),
            P("dp", "head", "seq"),
        ),
        out_specs=(P("dp", "seq", "head"), P(("seq", "dp"), "head")),
        check_vma=False,
    )
```
